32 devices in a mesh: lat: 16 (over z, y, core), seg: 2 (over x).
Axes of the slice: x: 2, y: 2, z: 4, core: 2. Of those that a mesh axis runs over, the one named last changes fastest.
Arguments:
- atmosphere: float32 [192, 96, 768], P('lat', 'seg'), may hold values from -6 to 6
- cloud_state: float32 [16, 96, 49152], P('lat', None, 'seg'), may hold values from -6 to 6
- channel_lat: int32 [16], P('lat'), may hold values from 0 to 191, as said below
- cell_column: int32 [16, 49152], P('lat', 'seg'), may hold values from 0 to 383, as said below
- channel_wind: float32 [16, 96], P('lat'), may hold values from -0.45 to 0.45
- diffusivity: float32 [96], replicated, may hold values from 0.03 to 0.25
- mixing: float32 [96, 96], replicated, may hold values from -0.625 to 0.625
Outputs:
- next_atmosphere: float32 [192, 96, 768], P('lat', 'seg')
- next_clouds: float32 [16, 96, 49152], P('lat', None, 'seg')
The draws below stay inside these ranges and needn't reach their ends.
Inputs may be any that keep to these rules, and one draw needn't show every extreme that they name: channel_lat[c] lies in the latitude rows c * 12 to (c + 1) * 12 - 1. `cell_column`: within each segment of 24576 cells of a channel, column numbers never fall and every column holds between half of 64 and three halves of 64 cells; both bounds are reached in every segment.
All inputs are finite; a program needn't handle non-finite values.
Results may differ from the reference program's by a relative error of at most 0.0003.
Values sent between devices are 32-bit elements; how exact they have to be, the bound alone decides.
A program may use at most 128 MiB of HBM per device.

```python
import math
import jax
import jax.numpy as jnp
from jax import lax

NLON = 768
M = 256
NT = 256
CPC = 64
LAT_DEV = 12
STEPS = 2
SUBSTEPS = 3
K = 96
NLAT = 192
CHANNELS = 16
COLS_SEG = 384
CELLS_SEG = 24576
CELLS = 49152
N_SEG = 2


def draw_channel_lat(key, part):
    offsets = jax.random.randint(key, (CHANNELS,), 0, LAT_DEV)
    offsets = offsets.at[0].set(0)
    offsets = offsets.at[CHANNELS - 1].set(LAT_DEV - 1)
    return (jnp.arange(CHANNELS, dtype=jnp.int32) * LAT_DEV + offsets).astype(jnp.int32)


def draw_cell_column(key, part):
    segments = CELLS // CELLS_SEG
    blocks = CHANNELS * segments
    pair_count = COLS_SEG // 2
    shift_key, order_key = jax.random.split(key)
    shifts = jax.random.randint(shift_key, (blocks, pair_count), -1, 2) * (CPC // 2)
    shifts = shifts.at[:, 0].set(CPC // 2)
    by_slot = jnp.concatenate((CPC + shifts, CPC - shifts), axis=1)
    orders = jax.vmap(lambda subkey: jax.random.permutation(subkey, COLS_SEG))(jax.random.split(order_key, blocks))
    counts = jnp.zeros((blocks, COLS_SEG), jnp.int32).at[jnp.arange(blocks)[:, None], orders].set(by_slot)
    bounds = jnp.cumsum(counts, axis=1)
    cells = jnp.arange(CELLS_SEG, dtype=jnp.int32)
    column = jax.vmap(lambda limits: jnp.searchsorted(limits, cells, side='right'))(bounds)
    return column.reshape(CHANNELS, segments * CELLS_SEG).astype(jnp.int32)


def block_levels(rng, shape, cuts, smallest, largest):
    loudness = 1.0
    for dim, shards_of in cuts:
        draws = jax.random.uniform(jax.random.fold_in(jax.random.fold_in(rng, 6), dim), (shards_of,), jnp.float32, smallest / len(cuts), largest / len(cuts))
        loudness = loudness * jnp.repeat(jnp.exp(draws), shape[dim] // shards_of).reshape((-1,) + (1,) * (len(shape) - 1 - dim))
    return loudness


def normal_values(own_key, extent, deviation, most, pieces=(), held_as=jnp.bfloat16):
    values = deviation * jax.random.normal(own_key, extent, jnp.float32)
    if pieces:
        values = values * block_levels(own_key, extent, pieces, -0.22, 0.18)
    return jnp.clip(values, -most, most).astype(held_as)


def setup_inputs(seed: int = 0) -> dict:
    arg_keys = jax.random.split(jax.random.key(seed), 8)
    return {
        "atmosphere": normal_values(arg_keys[0], (NLAT, K, NLON), 1.0, 6.0, ((0, 16), (1, 2)), jnp.float32),
        "cloud_state": normal_values(arg_keys[1], (CHANNELS, K, CELLS), 1.0, 6.0, ((0, 16), (2, 2)), jnp.float32),
        "channel_lat": draw_channel_lat(jax.random.fold_in(arg_keys[7], 71), 0),
        "cell_column": draw_cell_column(jax.random.fold_in(arg_keys[7], 71), 0),
        "channel_wind": jnp.clip(jax.random.uniform(arg_keys[4], (CHANNELS, K), jnp.float32, -0.45, 0.45) * block_levels(arg_keys[4], (CHANNELS, K), ((0, 16),), -0.4, 0.0), -0.45, 0.45),
        "diffusivity": jnp.clip(jnp.exp(jax.random.uniform(arg_keys[5], (K,), jnp.float32, math.log(0.03), math.log(0.25))), 0.03, 0.25),
        "mixing": normal_values(arg_keys[6], (K, K), K ** -0.5, 0.625, (), jnp.float32),
    }


RELAXATION = 0.5
MIXING_RATE = 0.3
DAMPING = 0.2
COUPLING = 2.0
HIGHEST = lax.Precision.HIGHEST


def fourier_tables(wavenumbers, longitudes):
    positions = jnp.arange(longitudes, dtype=jnp.int32)
    phase_turns = (positions[:, None] * wavenumbers[None, :]) % longitudes
    angles = phase_turns.astype(jnp.float32) * (2.0 * math.pi / longitudes)
    waves_pair = jnp.stack((jnp.cos(angles), jnp.sin(angles)), axis=2)
    weights = jnp.where(wavenumbers == 0, 1.0, 2.0).astype(jnp.float32)
    return waves_pair / longitudes, waves_pair * weights[None, :, None]


def meridian_tables(latitudes, degrees, lat_total):
    phase_turns = (degrees[:, None] * (2 * latitudes[None, :] + 1)) % (4 * lat_total)
    angles = phase_turns.astype(jnp.float32) * (math.pi / (2.0 * lat_total))
    basis = jnp.cos(angles)
    weights = jnp.where(degrees == 0, 1.0, 2.0).astype(jnp.float32) / lat_total
    return basis * weights[:, None], jnp.transpose(basis)


def implicit_solve(spectrum, wavenumbers):
    degree_total = spectrum.shape[0]
    degrees = jnp.arange(degree_total, dtype=jnp.int32)
    wave_values = wavenumbers.astype(jnp.float32)
    degree_values = degrees.astype(jnp.float32)
    size_ratio = (wave_values[None, :] * wave_values[None, :] + degree_values[:, None] * degree_values[:, None]) / (degree_total * degree_total)
    damping_factor = (1.0 + size_ratio * size_ratio)[:, :, None, None]
    coupling_factor = (COUPLING * size_ratio)[:, :, None, None]
    determinant = damping_factor * damping_factor + coupling_factor * coupling_factor
    retained = ((wavenumbers[None, :] + degrees[:, None]) < degree_total).astype(jnp.float32)[:, :, None, None, None]
    shape_full = spectrum.shape
    components = spectrum.reshape(shape_full[0], shape_full[1], shape_full[2], shape_full[3] // 3, 3)
    vorticity = components[..., 0] / damping_factor
    divergence = (damping_factor * components[..., 1] + coupling_factor * components[..., 2]) / determinant
    geopotential = (damping_factor * components[..., 2] - coupling_factor * components[..., 1]) / determinant
    return (jnp.stack((vorticity, divergence, geopotential), axis=4) * retained).reshape(shape_full)


def advance(padded, forcing, diffusivity, channel_wind, mixing):
    center = padded[:, :, 1:-1]
    right_cell = padded[:, :, 2:]
    left_cell = padded[:, :, :-2]
    mixed_levels = jnp.einsum("kl,clx->ckx", mixing, center, precision=HIGHEST)
    return (center + diffusivity[None, :, None] * (right_cell - 2.0 * center + left_cell)
            - 0.5 * channel_wind[:, :, None] * (right_cell - left_cell)
            + MIXING_RATE * mixed_levels + forcing - DAMPING * jnp.tanh(center))


def channel_step(clouds, column, wind_row, profile, diffusivity, mixing):
    local_cells = column.reshape(N_SEG, CELLS_SEG)
    onehot = (local_cells[:, :, None] == jnp.arange(COLS_SEG, dtype=jnp.int32)[None, None, :]).astype(jnp.float32)
    counts = jnp.sum(onehot, axis=1)

    def column_mean(values):
        column_sums = jnp.einsum("ksx,sxn->ksn", values.reshape(K, N_SEG, CELLS_SEG), onehot, precision=HIGHEST)
        return (column_sums / counts[None]).reshape(K, NLON)

    start_mean = column_mean(clouds)
    pulled = RELAXATION * (profile - start_mean)
    forcing = jnp.einsum("ksn,sxn->ksx", pulled.reshape(K, N_SEG, COLS_SEG), onehot, precision=HIGHEST).reshape(1, K, CELLS)
    cloud_now = clouds[None]
    for substep in range(SUBSTEPS):
        padded = jnp.concatenate((cloud_now[:, :, -1:], cloud_now, cloud_now[:, :, :1]), axis=2)
        cloud_now = advance(padded, forcing, diffusivity, wind_row[None], mixing)
    return cloud_now[0], column_mean(cloud_now[0]) - start_mean


def reference(atmosphere, cloud_state, channel_lat, cell_column, channel_wind, diffusivity, mixing):
    wavenumbers = jnp.arange(M, dtype=jnp.int32)
    forward, inverse = fourier_tables(wavenumbers, NLON)
    to_spec, from_spec = meridian_tables(jnp.arange(NLAT, dtype=jnp.int32), jnp.arange(NT, dtype=jnp.int32), NLAT)
    for model_step in range(STEPS):
        profiles = jnp.take(atmosphere, channel_lat, axis=0)
        cloud_state, tendency = lax.map(
            lambda packed: channel_step(packed[0], packed[1], packed[2], packed[3], diffusivity, mixing),
            (cloud_state, cell_column, channel_wind, profiles))
        atmosphere = atmosphere.at[channel_lat].add(tendency)
        coeffs = jnp.einsum("jkx,xmc->jmck", atmosphere, forward, precision=HIGHEST)
        spectrum = jnp.einsum("nj,jmck->nmck", to_spec, coeffs, precision=HIGHEST)
        spectrum = implicit_solve(spectrum, wavenumbers)
        back_rows = jnp.einsum("jn,nmck->jmck", from_spec, spectrum, precision=HIGHEST)
        atmosphere = jnp.einsum("jmck,xmc->jkx", back_rows, inverse, precision=HIGHEST)
    return atmosphere, cloud_state
```

```python
import math

import jax
import jax.numpy as jnp
from jax import lax
from jax.experimental import pallas as pl
from jax.experimental.pallas import tpu as pltpu
from jax.sharding import PartitionSpec as P


M = 256
NT = 256

RELAXATION = 0.5
MIXING_RATE = 0.3
DAMPING = 0.2
COUPLING = 2.0
HIGHEST = lax.Precision.HIGHEST
HIGH = lax.Precision.HIGH

CHUNK = 256
TILE = 128
BAND = 32
BOTH = ("lat", "seg")


def fourier_tables(wavenumbers, positions, longitudes):
    phase_turns = positions[:, None] * wavenumbers[None, :] % longitudes
    angles = phase_turns.astype(jnp.float32) * (2.0 * math.pi / longitudes)
    return jnp.stack((jnp.cos(angles), jnp.sin(angles)), axis=2)


def forward_table(positions, longitudes):
    waves = jnp.arange(M, dtype=jnp.int32)
    pair = fourier_tables(waves, positions, longitudes) / longitudes
    return pair.reshape(positions.shape[0], M * 2)


def inverse_table(positions, longitudes):
    waves = jnp.arange(M, dtype=jnp.int32)
    weights = jnp.where(waves == 0, 1.0, 2.0).astype(jnp.float32)
    pair = fourier_tables(waves, positions, longitudes) * weights[None, :, None]
    return pair.reshape(positions.shape[0], M * 2)


def meridian_tables(latitudes, degrees, lat_total):
    phase_turns = degrees[:, None] * (2 * latitudes[None, :] + 1) % (4 * lat_total)
    angles = phase_turns.astype(jnp.float32) * (math.pi / (2.0 * lat_total))
    basis = jnp.cos(angles)
    weights = jnp.where(degrees == 0, 1.0, 2.0).astype(jnp.float32) / lat_total
    return (basis * weights[:, None], jnp.transpose(basis))


def implicit_solve(spectrum, first_wave, pairs):
    rows, width = spectrum.shape
    column = lax.broadcasted_iota(jnp.int32, (1, width), 1)
    wave = first_wave + column // (2 * pairs)
    variable = column % pairs % 3
    degree = lax.broadcasted_iota(jnp.int32, (rows, 1), 0)
    wave_value = wave.astype(jnp.float32)
    degree_value = degree.astype(jnp.float32)
    ratio = (wave_value * wave_value + degree_value * degree_value) / (rows * rows)
    damping = 1.0 + ratio * ratio
    coupling = COUPLING * ratio
    determinant = damping * damping + coupling * coupling
    after = jnp.concatenate((spectrum[:, 1:], spectrum[:, :1]), axis=1)
    before = jnp.concatenate((spectrum[:, -1:], spectrum[:, :-1]), axis=1)
    partner = jnp.where(variable == 1, after, -before)
    coupled = (damping * spectrum + coupling * partner) / determinant
    solved = jnp.where(variable == 0, spectrum / damping, coupled)
    return jnp.where(wave + degree < rows, solved, 0.0)


def halves(values):
    high = values.astype(jnp.bfloat16)
    low = (values - high.astype(jnp.float32)).astype(jnp.bfloat16)
    return high, low


def band_onehot(ids, base):
    rows = lax.broadcasted_iota(jnp.int32, (BAND, CHUNK), 0) + base
    return jnp.where(rows == ids, 1.0, 0.0).astype(jnp.bfloat16)


def add_band(sums_ref, base, onehot, stacked):
    part = lax.dot_general(
        onehot, stacked, (((1,), (1,)), ((), ())), preferred_element_type=jnp.float32
    )
    rows = pl.ds(base, BAND)
    sums_ref[rows, :] = sums_ref[rows, :] + part


def mean_kernel(base_ref, ids_ref, state_ref, sums_ref):
    step = pl.program_id(0)
    block = state_ref.shape[1]

    @pl.when(step == 0)
    def _():
        sums_ref[...] = jnp.zeros_like(sums_ref)

    ones = jnp.ones((sums_ref.shape[1] - 2 * state_ref.shape[0], CHUNK), jnp.bfloat16)
    for chunk in range(block // CHUNK):
        start = pl.multiple_of(step * block + TILE + chunk * CHUNK, TILE)
        base = pl.multiple_of(base_ref[step * (block // TILE) + 1 + chunk * (CHUNK // TILE)], 8)
        onehot = band_onehot(ids_ref[:, pl.ds(start, CHUNK)], base)
        high, low = halves(state_ref[:, chunk * CHUNK : (chunk + 1) * CHUNK])
        add_band(sums_ref, base, onehot, jnp.concatenate((high, low, ones), axis=0))


def cloud_kernel(
    base_ref, ids_ref, main_ref, left_ref, right_ref, halo_left_ref, halo_right_ref,
    pulled_ref, mix_ref, own_ref, up_ref, down_ref, next_ref, sums_ref, one, two, force,
):
    step = pl.program_id(0)
    count = pl.num_programs(0)
    pairs, block = main_ref.shape

    @pl.when(step == 0)
    def _():
        sums_ref[...] = jnp.zeros_like(sums_ref)
        one[:, TILE : 2 * TILE] = halo_left_ref[...]

    @pl.when(step > 0)
    def _():
        one[:, TILE : 2 * TILE] = left_ref[...]

    @pl.when(step == count - 1)
    def _():
        one[:, 2 * TILE + block : 3 * TILE + block] = halo_right_ref[...]

    @pl.when(step < count - 1)
    def _():
        one[:, 2 * TILE + block : 3 * TILE + block] = right_ref[...]

    one[:, 2 * TILE : 2 * TILE + block] = main_ref[...]
    mix = mix_ref[...]

    def first_base(offset):
        return pl.multiple_of(base_ref[step * (block // TILE) + offset // TILE], 8)

    def chunk_ids(offset):
        return ids_ref[:, pl.ds(pl.multiple_of(step * block + offset, TILE), CHUNK)]

    def advanced(source, offset, forcing):
        at = TILE + offset
        center = source[:, at : at + CHUNK]
        wide = source[:, at - TILE : at + CHUNK + TILE]
        span = CHUNK + 2 * TILE
        right_cell = pltpu.roll(wide, span - 1, 1)[:, TILE : TILE + CHUNK]
        left_cell = pltpu.roll(wide, 1, 1)[:, TILE : TILE + CHUNK]
        mixed = jnp.dot(
            mix, jnp.concatenate(halves(center), axis=0), preferred_element_type=jnp.float32
        )
        return (
            own_ref[...] * center
            + up_ref[...] * right_cell
            + down_ref[...] * left_cell
            + (mixed[:pairs] + mixed[pairs:])
            + forcing
            - DAMPING * jnp.tanh(center)
        )

    wide_chunks = (block + 2 * TILE) // CHUNK
    for chunk in range(wide_chunks):
        offset = chunk * CHUNK
        base = first_base(offset)
        onehot = band_onehot(chunk_ids(offset), base)
        band = jnp.concatenate(halves(pulled_ref[pl.ds(base, BAND), :]), axis=0)
        forcing = lax.dot_general(
            band,
            jnp.concatenate((onehot, onehot), axis=0),
            (((0,), (0,)), ((), ())),
            preferred_element_type=jnp.float32,
        )
        force[:, offset : offset + CHUNK] = forcing
        two[:, TILE + offset : TILE + offset + CHUNK] = advanced(one, offset, forcing)
    for chunk in range(wide_chunks):
        offset = chunk * CHUNK
        forcing = force[:, offset : offset + CHUNK]
        one[:, TILE + offset : TILE + offset + CHUNK] = advanced(two, offset, forcing)
    for chunk in range(block // CHUNK):
        offset = TILE + chunk * CHUNK
        fresh = advanced(one, offset, force[:, offset : offset + CHUNK])
        next_ref[:, chunk * CHUNK : (chunk + 1) * CHUNK] = fresh
        base = first_base(offset)
        onehot = band_onehot(chunk_ids(offset), base)
        add_band(sums_ref, base, onehot, jnp.concatenate(halves(fresh), axis=0))


def block_size(cells):
    for size in (3072, 2048, 1024, 512):
        if cells % size == 0:
            return size
    return CHUNK


def whole(shape):
    return pl.BlockSpec(shape, lambda i, base: (0,) * len(shape))


def column_sums(clouds, ids, bases, rows):
    pairs, cells = clouds.shape
    block = block_size(cells)
    width = 2 * pairs + 64
    return pl.pallas_call(
        mean_kernel,
        out_shape=jax.ShapeDtypeStruct((rows, width), jnp.float32),
        grid_spec=pltpu.PrefetchScalarGridSpec(
            num_scalar_prefetch=1,
            grid=(cells // block,),
            in_specs=[whole(ids.shape), pl.BlockSpec((pairs, block), lambda i, base: (0, i))],
            out_specs=whole((rows, width)),
        ),
        name="column_sums",
    )(bases, ids, clouds)


def cloud_step(clouds, halo_left, halo_right, ids, bases, pulled, mix, own, up, down):
    pairs, cells = clouds.shape
    block = block_size(cells)
    tiles = block // TILE
    last = cells // TILE - 1
    rows = pulled.shape[0]
    wide = block + 4 * TILE
    return pl.pallas_call(
        cloud_kernel,
        out_shape=(
            jax.ShapeDtypeStruct((pairs, cells), jnp.float32),
            jax.ShapeDtypeStruct((rows, 2 * pairs), jnp.float32),
        ),
        grid_spec=pltpu.PrefetchScalarGridSpec(
            num_scalar_prefetch=1,
            grid=(cells // block,),
            in_specs=[
                whole(ids.shape),
                pl.BlockSpec((pairs, block), lambda i, base: (0, i)),
                pl.BlockSpec((pairs, TILE), lambda i, base: (0, jnp.maximum(i * tiles - 1, 0))),
                pl.BlockSpec((pairs, TILE), lambda i, base: (0, jnp.minimum((i + 1) * tiles, last))),
                whole((pairs, TILE)),
                whole((pairs, TILE)),
                whole((rows, pairs)),
                whole((2 * pairs, 2 * pairs)),
                whole((pairs, CHUNK)),
                whole((pairs, CHUNK)),
                whole((pairs, CHUNK)),
            ],
            out_specs=[
                pl.BlockSpec((pairs, block), lambda i, base: (0, i)),
                whole((rows, 2 * pairs)),
            ],
            scratch_shapes=[
                pltpu.VMEM((pairs, wide), jnp.float32),
                pltpu.VMEM((pairs, wide), jnp.float32),
                pltpu.VMEM((pairs, block + 2 * TILE), jnp.float32),
            ],
        ),
        name="cloud_step",
    )(bases, ids, clouds, clouds, clouds, halo_left, halo_right, pulled, mix, own, up, down)


def whole_run(
    atmosphere, cloud_state, channel_lat, cell_column, channel_wind, diffusivity, mixing
):
    lat_dev, pairs_here, longitudes = atmosphere.shape
    lat_count = lax.axis_size("lat")
    seg_count = lax.axis_size("seg")
    lat_index = lax.axis_index("lat")
    seg_index = lax.axis_index("seg")
    devices = lat_count * seg_count
    lat_total = lat_dev * lat_count
    columns = longitudes // seg_count
    owned = M // lat_count
    flat = owned * 2 * pairs_here
    pairs = pairs_here * seg_count
    degrees = jnp.arange(NT, dtype=jnp.int32)
    to_spec, from_spec = meridian_tables(jnp.arange(lat_total, dtype=jnp.int32), degrees, lat_total)
    offset = channel_lat[0] - lat_index * lat_dev
    clouds = cloud_state[0]

    forward_ring = [(i, (i + 1) % seg_count) for i in range(seg_count)]
    backward_ring = [(target, source) for source, target in forward_ring]

    def edges(block):
        low = lax.ppermute(block[:, -TILE:], "seg", forward_ring)
        high = lax.ppermute(block[:, :TILE], "seg", backward_ring)
        return low, high

    row = lax.dynamic_slice_in_dim(atmosphere, offset, 1, axis=0)[0]
    around = jnp.concatenate((row[:, -1:], row, row[:, :1]), axis=1)
    pieces = jnp.stack([around[:, s * columns : (s + 1) * columns + 2] for s in range(seg_count)])
    profile = lax.all_to_all(pieces, "seg", split_axis=0, concat_axis=0, tiled=True)
    profile = jnp.transpose(profile.reshape(pairs, columns + 2))

    low_column, high_column = edges(cell_column)
    low_mask = (low_column == columns - 1).astype(jnp.float32)
    high_mask = (high_column == 0).astype(jnp.float32)
    low_count = jnp.sum(low_mask)
    high_count = jnp.sum(high_mask)

    ids = jnp.concatenate(
        (
            jnp.zeros((1, TILE), jnp.int32),
            cell_column + 1,
            jnp.full((1, TILE), columns + 1, jnp.int32),
        ),
        axis=1,
    )
    bases = ids[0, ::TILE] // 8 * 8
    rows = (columns + 2 + 7) // 8 * 8 + BAND

    def mean_of(sums, counts):
        return (sums[1 : columns + 1, :pairs] + sums[1 : columns + 1, pairs : 2 * pairs]) / counts

    first = column_sums(clouds, ids, bases, rows)
    counts = first[1 : columns + 1, 2 * pairs : 2 * pairs + 1]
    start = mean_of(first, counts)

    table = forward_table(jnp.arange(longitudes, dtype=jnp.int32), longitudes)
    coeff_rows = jnp.einsum("jkx,xn->jnk", atmosphere, table, precision=HIGH)
    coeff_flat = coeff_rows.reshape(lat_dev, M * 2 * pairs_here)
    gathered = lax.all_to_all(coeff_flat, "lat", split_axis=1, concat_axis=0, tiled=True)
    base_spectrum = jnp.dot(to_spec, gathered, precision=HIGH)

    wind = channel_wind[0]
    spread = (pairs, CHUNK)
    own = jnp.broadcast_to((1.0 - 2.0 * diffusivity)[:, None], spread)
    up = jnp.broadcast_to((diffusivity - 0.5 * wind)[:, None], spread)
    down = jnp.broadcast_to((diffusivity + 0.5 * wind)[:, None], spread)
    scaled = MIXING_RATE * mixing
    mix_high = lax.reduce_precision(scaled, 8, 7)
    mix_low = scaled - mix_high
    mix = jnp.concatenate(
        (
            jnp.concatenate((mix_high, mix_high), axis=1),
            jnp.concatenate((mix_low, mix_low), axis=1),
        ),
        axis=0,
    ).astype(jnp.bfloat16)

    local_table = forward_table(
        seg_index * columns + jnp.arange(columns, dtype=jnp.int32), longitudes
    )
    local_inverse = inverse_table(
        (seg_index * columns - 1 + longitudes + jnp.arange(columns + 2, dtype=jnp.int32))
        % longitudes,
        longitudes,
    )

    def run_clouds(clouds, halo_low, halo_high, profile, start):
        low_mean = jnp.sum(halo_low * low_mask, axis=1) / low_count
        high_mean = jnp.sum(halo_high * high_mask, axis=1) / high_count
        start_wide = jnp.concatenate((low_mean[None], start, high_mean[None]), axis=0)
        pulled = RELAXATION * (profile - start_wide)
        pulled = jnp.pad(pulled, ((0, rows - columns - 2), (0, 0)))
        clouds, sums = cloud_step(
            clouds, halo_low, halo_high, ids, bases, pulled, mix, own, up, down
        )
        return clouds, mean_of(sums, counts)

    def sent_tendency(tendency):
        coeffs = jnp.einsum("xn,xk->nk", local_table, tendency, precision=HIGH)
        coeffs = coeffs.reshape(lat_count, owned * 2, seg_count, pairs_here)
        return jnp.transpose(coeffs, (0, 2, 1, 3)).reshape(devices, flat)

    halo_low, halo_high = edges(clouds)
    clouds, after = run_clouds(clouds, halo_low, halo_high, profile, start)
    halo_low, halo_high = edges(clouds)
    sent = sent_tendency(after - start)
    mark = jnp.broadcast_to(channel_lat.astype(jnp.float32)[None, :], (devices, TILE))
    received = lax.all_to_all(
        jnp.concatenate((sent, mark), axis=1), BOTH, split_axis=0, concat_axis=0, tiled=True
    )
    source_lat = received[:, flat].astype(jnp.int32)
    to_rows, from_rows = meridian_tables(source_lat, degrees, lat_total)
    spectrum = base_spectrum + jnp.dot(to_rows, received[:, :flat], precision=HIGHEST)
    spectrum = implicit_solve(spectrum, lat_index * owned, pairs_here)

    channel_coeffs = jnp.dot(from_rows, spectrum, precision=HIGHEST)
    arrived = lax.all_to_all(channel_coeffs, BOTH, split_axis=0, concat_axis=0, tiled=True)
    arrived = arrived.reshape(lat_count, seg_count, owned * 2, pairs_here)
    arrived = jnp.transpose(arrived, (0, 2, 1, 3)).reshape(M * 2, pairs)
    profile = jnp.dot(local_inverse, arrived, precision=HIGH)
    there_and_back = jnp.dot(to_spec, from_spec, precision=HIGHEST)
    base_spectrum = jnp.dot(there_and_back, spectrum, precision=HIGH)

    start = after
    clouds, after = run_clouds(clouds, halo_low, halo_high, profile, start)
    received = lax.all_to_all(
        sent_tendency(after - start), BOTH, split_axis=0, concat_axis=0, tiled=True
    )
    spectrum = base_spectrum + jnp.dot(to_rows, received, precision=HIGHEST)
    spectrum = implicit_solve(spectrum, lat_index * owned, pairs_here)
    back_rows = jnp.dot(from_spec, spectrum, precision=HIGH)
    restored = lax.all_to_all(back_rows, "lat", split_axis=0, concat_axis=1, tiled=True)
    inverse = inverse_table(jnp.arange(longitudes, dtype=jnp.int32), longitudes)
    atmosphere = jnp.einsum(
        "jnk,xn->jkx", restored.reshape(lat_dev, M * 2, pairs_here), inverse, precision=HIGH
    )
    return (atmosphere, clouds[None])


def solution(mesh):
    placed = (
        P("lat", "seg", None),
        P("lat", None, "seg"),
        P("lat"),
        P("lat", "seg"),
        P("lat", None),
        P(),
        P(),
    )
    return jax.shard_map(
        whole_run,
        mesh=mesh,
        in_specs=placed,
        out_specs=(P("lat", "seg", None), P("lat", None, "seg")),
        check_vma=False,
    )
```

```python
import math

import jax
import jax.numpy as jnp
import numpy as np
from jax import lax
from jax.experimental import pallas as pl
from jax.experimental.pallas import tpu as pltpu
from jax.sharding import PartitionSpec as P


M = 256
NT = 256

RELAXATION = 0.5
MIXING_RATE = 0.3
DAMPING = 0.2
COUPLING = 2.0
HIGHEST = lax.Precision.HIGHEST
HIGH = lax.Precision.HIGH

CHUNK = 256
TILE = 128
BAND = 32
BOTH = ("lat", "seg")


def fourier_tables(positions, longitudes):
    waves = np.arange(M)
    angles = (positions[:, None] * waves[None, :] % longitudes) * (2.0 * math.pi / longitudes)
    pair = np.stack((np.cos(angles), np.sin(angles)), axis=2)
    weights = np.where(waves == 0, 1.0, 2.0)
    forward = (pair / longitudes).reshape(positions.shape[0], M * 2)
    inverse = (pair * weights[None, :, None]).reshape(positions.shape[0], M * 2)
    return forward.astype(np.float32), inverse.astype(np.float32)


def fixed_meridian_tables(degree_total, lat_total):
    degrees = np.arange(degree_total)
    turns = degrees[:, None] * (2 * np.arange(lat_total)[None, :] + 1) % (4 * lat_total)
    basis = np.cos(turns * (math.pi / (2.0 * lat_total)))
    weights = np.where(degrees == 0, 1.0, 2.0) / lat_total
    to_spec = basis * weights[:, None]
    from_spec = np.transpose(basis)
    return tuple(t.astype(np.float32) for t in (to_spec, from_spec, to_spec @ from_spec))


def meridian_tables(latitudes, degrees, lat_total):
    phase_turns = degrees[:, None] * (2 * latitudes[None, :] + 1) % (4 * lat_total)
    angles = phase_turns.astype(jnp.float32) * (math.pi / (2.0 * lat_total))
    basis = jnp.cos(angles)
    weights = jnp.where(degrees == 0, 1.0, 2.0).astype(jnp.float32) / lat_total
    return (basis * weights[:, None], jnp.transpose(basis))


def implicit_solve(spectrum, first_wave, pairs):
    rows, width = spectrum.shape
    column = lax.broadcasted_iota(jnp.int32, (1, width), 1)
    wave = first_wave + column // (2 * pairs)
    variable = column % pairs % 3
    degree = lax.broadcasted_iota(jnp.int32, (rows, 1), 0)
    wave_value = wave.astype(jnp.float32)
    degree_value = degree.astype(jnp.float32)
    ratio = (wave_value * wave_value + degree_value * degree_value) / (rows * rows)
    damping = 1.0 + ratio * ratio
    coupling = COUPLING * ratio
    determinant = damping * damping + coupling * coupling
    after = jnp.concatenate((spectrum[:, 1:], spectrum[:, :1]), axis=1)
    before = jnp.concatenate((spectrum[:, -1:], spectrum[:, :-1]), axis=1)
    partner = jnp.where(variable == 1, after, -before)
    coupled = (damping * spectrum + coupling * partner) / determinant
    solved = jnp.where(variable == 0, spectrum / damping, coupled)
    return jnp.where(wave + degree < rows, solved, 0.0)


def halves(values):
    high = values.astype(jnp.bfloat16)
    low = (values - high.astype(jnp.float32)).astype(jnp.bfloat16)
    return high, low


def band_onehot(ids, base):
    rows = lax.broadcasted_iota(jnp.int32, (BAND, CHUNK), 0) + base
    return jnp.where(rows == ids, 1.0, 0.0).astype(jnp.bfloat16)


def add_band(sums_ref, base, onehot, stacked):
    part = lax.dot_general(
        onehot, stacked, (((1,), (1,)), ((), ())), preferred_element_type=jnp.float32
    )
    rows = pl.ds(base, BAND)
    sums_ref[rows, :] = sums_ref[rows, :] + part


def mean_kernel(base_ref, ids_ref, state_ref, sums_ref):
    step = pl.program_id(0)
    block = state_ref.shape[1]

    @pl.when(step == 0)
    def _():
        sums_ref[...] = jnp.zeros_like(sums_ref)

    ones = jnp.ones((sums_ref.shape[1] - 2 * state_ref.shape[0], CHUNK), jnp.bfloat16)
    for chunk in range(block // CHUNK):
        start = pl.multiple_of(step * block + TILE + chunk * CHUNK, TILE)
        base = pl.multiple_of(base_ref[step * (block // TILE) + 1 + chunk * (CHUNK // TILE)], 8)
        onehot = band_onehot(ids_ref[:, pl.ds(start, CHUNK)], base)
        high, low = halves(state_ref[:, chunk * CHUNK : (chunk + 1) * CHUNK])
        add_band(sums_ref, base, onehot, jnp.concatenate((high, low, ones), axis=0))


def cloud_kernel(
    base_ref, ids_ref, main_ref, left_ref, right_ref, halo_left_ref, halo_right_ref,
    pulled_ref, mix_ref, own_ref, up_ref, down_ref, next_ref, sums_ref, one, two, force,
):
    step = pl.program_id(0)
    count = pl.num_programs(0)
    pairs, block = main_ref.shape

    @pl.when(step == 0)
    def _():
        sums_ref[...] = jnp.zeros_like(sums_ref)
        one[:, TILE : 2 * TILE] = halo_left_ref[...]

    @pl.when(step > 0)
    def _():
        one[:, TILE : 2 * TILE] = left_ref[...]

    @pl.when(step == count - 1)
    def _():
        one[:, 2 * TILE + block : 3 * TILE + block] = halo_right_ref[...]

    @pl.when(step < count - 1)
    def _():
        one[:, 2 * TILE + block : 3 * TILE + block] = right_ref[...]

    one[:, 2 * TILE : 2 * TILE + block] = main_ref[...]
    mix = mix_ref[...]

    def first_base(offset):
        return pl.multiple_of(base_ref[step * (block // TILE) + offset // TILE], 8)

    def chunk_ids(offset):
        return ids_ref[:, pl.ds(pl.multiple_of(step * block + offset, TILE), CHUNK)]

    def advanced(source, offset, forcing):
        at = TILE + offset
        center = source[:, at : at + CHUNK]
        wide = source[:, at - TILE : at + CHUNK + TILE]
        span = CHUNK + 2 * TILE
        right_cell = pltpu.roll(wide, span - 1, 1)[:, TILE : TILE + CHUNK]
        left_cell = pltpu.roll(wide, 1, 1)[:, TILE : TILE + CHUNK]
        mixed = jnp.dot(
            mix, jnp.concatenate(halves(center), axis=0), preferred_element_type=jnp.float32
        )
        return (
            own_ref[...] * center
            + up_ref[...] * right_cell
            + down_ref[...] * left_cell
            + (mixed[:pairs] + mixed[pairs:])
            + forcing
            - DAMPING * jnp.tanh(center)
        )

    wide_chunks = (block + 2 * TILE) // CHUNK
    for chunk in range(wide_chunks):
        offset = chunk * CHUNK
        base = first_base(offset)
        onehot = band_onehot(chunk_ids(offset), base)
        band = jnp.concatenate(halves(pulled_ref[pl.ds(base, BAND), :]), axis=0)
        forcing = lax.dot_general(
            band,
            jnp.concatenate((onehot, onehot), axis=0),
            (((0,), (0,)), ((), ())),
            preferred_element_type=jnp.float32,
        )
        force[:, offset : offset + CHUNK] = forcing
        two[:, TILE + offset : TILE + offset + CHUNK] = advanced(one, offset, forcing)
    for chunk in range(wide_chunks):
        offset = chunk * CHUNK
        forcing = force[:, offset : offset + CHUNK]
        one[:, TILE + offset : TILE + offset + CHUNK] = advanced(two, offset, forcing)
    for chunk in range(block // CHUNK):
        offset = TILE + chunk * CHUNK
        fresh = advanced(one, offset, force[:, offset : offset + CHUNK])
        next_ref[:, chunk * CHUNK : (chunk + 1) * CHUNK] = fresh
        base = first_base(offset)
        onehot = band_onehot(chunk_ids(offset), base)
        add_band(sums_ref, base, onehot, jnp.concatenate(halves(fresh), axis=0))


def block_size(cells):
    for size in (3072, 2048, 1024, 512):
        if cells % size == 0:
            return size
    return CHUNK


def whole(shape):
    return pl.BlockSpec(shape, lambda i, base: (0,) * len(shape))


def column_sums(clouds, ids, bases, rows):
    pairs, cells = clouds.shape
    block = block_size(cells)
    width = 2 * pairs + 64
    return pl.pallas_call(
        mean_kernel,
        out_shape=jax.ShapeDtypeStruct((rows, width), jnp.float32),
        grid_spec=pltpu.PrefetchScalarGridSpec(
            num_scalar_prefetch=1,
            grid=(cells // block,),
            in_specs=[whole(ids.shape), pl.BlockSpec((pairs, block), lambda i, base: (0, i))],
            out_specs=whole((rows, width)),
        ),
        name="column_sums",
    )(bases, ids, clouds)


def cloud_step(clouds, halo_left, halo_right, ids, bases, pulled, mix, own, up, down):
    pairs, cells = clouds.shape
    block = block_size(cells)
    tiles = block // TILE
    last = cells // TILE - 1
    rows = pulled.shape[0]
    wide = block + 4 * TILE
    return pl.pallas_call(
        cloud_kernel,
        out_shape=(
            jax.ShapeDtypeStruct((pairs, cells), jnp.float32),
            jax.ShapeDtypeStruct((rows, 2 * pairs), jnp.float32),
        ),
        grid_spec=pltpu.PrefetchScalarGridSpec(
            num_scalar_prefetch=1,
            grid=(cells // block,),
            in_specs=[
                whole(ids.shape),
                pl.BlockSpec((pairs, block), lambda i, base: (0, i)),
                pl.BlockSpec((pairs, TILE), lambda i, base: (0, jnp.maximum(i * tiles - 1, 0))),
                pl.BlockSpec((pairs, TILE), lambda i, base: (0, jnp.minimum((i + 1) * tiles, last))),
                whole((pairs, TILE)),
                whole((pairs, TILE)),
                whole((rows, pairs)),
                whole((2 * pairs, 2 * pairs)),
                whole((pairs, CHUNK)),
                whole((pairs, CHUNK)),
                whole((pairs, CHUNK)),
            ],
            out_specs=[
                pl.BlockSpec((pairs, block), lambda i, base: (0, i)),
                whole((rows, 2 * pairs)),
            ],
            scratch_shapes=[
                pltpu.VMEM((pairs, wide), jnp.float32),
                pltpu.VMEM((pairs, wide), jnp.float32),
                pltpu.VMEM((pairs, block + 2 * TILE), jnp.float32),
            ],
        ),
        name="cloud_step",
    )(bases, ids, clouds, clouds, clouds, halo_left, halo_right, pulled, mix, own, up, down)


def whole_run(
    atmosphere, cloud_state, channel_lat, cell_column, channel_wind, diffusivity, mixing
):
    lat_dev, pairs_here, longitudes = atmosphere.shape
    lat_count = lax.axis_size("lat")
    seg_count = lax.axis_size("seg")
    lat_index = lax.axis_index("lat")
    seg_index = lax.axis_index("seg")
    devices = lat_count * seg_count
    lat_total = lat_dev * lat_count
    columns = longitudes // seg_count
    owned = M // lat_count
    flat = owned * 2 * pairs_here
    pairs = pairs_here * seg_count
    degrees = jnp.arange(NT, dtype=jnp.int32)
    to_spec, from_spec, there_and_back = (
        jnp.asarray(t) for t in fixed_meridian_tables(NT, lat_total)
    )
    forward, inverse = (jnp.asarray(t) for t in fourier_tables(np.arange(longitudes), longitudes))
    around_inverse = jnp.asarray(fourier_tables(np.arange(-1, longitudes + 1), longitudes)[1])
    offset = channel_lat[0] - lat_index * lat_dev
    clouds = cloud_state[0]

    forward_ring = [(i, (i + 1) % seg_count) for i in range(seg_count)]
    backward_ring = [(target, source) for source, target in forward_ring]

    def edges(block):
        low = lax.ppermute(block[:, -TILE:], "seg", forward_ring)
        high = lax.ppermute(block[:, :TILE], "seg", backward_ring)
        return low, high

    row = lax.dynamic_slice_in_dim(atmosphere, offset, 1, axis=0)[0]
    around = jnp.concatenate((row[:, -1:], row, row[:, :1]), axis=1)
    pieces = jnp.stack([around[:, s * columns : (s + 1) * columns + 2] for s in range(seg_count)])
    profile = lax.all_to_all(pieces, "seg", split_axis=0, concat_axis=0, tiled=True)
    profile = jnp.transpose(profile.reshape(pairs, columns + 2))

    low_column, high_column = edges(cell_column)
    low_mask = (low_column == columns - 1).astype(jnp.float32)
    high_mask = (high_column == 0).astype(jnp.float32)
    low_count = jnp.sum(low_mask)
    high_count = jnp.sum(high_mask)

    ids = jnp.concatenate(
        (
            jnp.zeros((1, TILE), jnp.int32),
            cell_column + 1,
            jnp.full((1, TILE), columns + 1, jnp.int32),
        ),
        axis=1,
    )
    bases = ids[0, ::TILE] // 8 * 8
    rows = (columns + 2 + 7) // 8 * 8 + BAND

    def mean_of(sums, counts):
        return (sums[1 : columns + 1, :pairs] + sums[1 : columns + 1, pairs : 2 * pairs]) / counts

    first = column_sums(clouds, ids, bases, rows)
    counts = first[1 : columns + 1, 2 * pairs : 2 * pairs + 1]
    start = mean_of(first, counts)

    coeff_rows = jnp.einsum("jkx,xn->jnk", atmosphere, forward, precision=HIGH)
    coeff_flat = coeff_rows.reshape(lat_dev, M * 2 * pairs_here)
    gathered = lax.all_to_all(coeff_flat, "lat", split_axis=1, concat_axis=0, tiled=True)
    base_spectrum = jnp.dot(to_spec, gathered, precision=HIGH)

    wind = channel_wind[0]
    spread = (pairs, CHUNK)
    own = jnp.broadcast_to((1.0 - 2.0 * diffusivity)[:, None], spread)
    up = jnp.broadcast_to((diffusivity - 0.5 * wind)[:, None], spread)
    down = jnp.broadcast_to((diffusivity + 0.5 * wind)[:, None], spread)
    scaled = MIXING_RATE * mixing
    mix_high = lax.reduce_precision(scaled, 8, 7)
    mix_low = scaled - mix_high
    mix = jnp.concatenate(
        (
            jnp.concatenate((mix_high, mix_high), axis=1),
            jnp.concatenate((mix_low, mix_low), axis=1),
        ),
        axis=0,
    ).astype(jnp.bfloat16)

    local_table = lax.dynamic_slice_in_dim(forward, seg_index * columns, columns, axis=0)
    local_inverse = lax.dynamic_slice_in_dim(
        around_inverse, seg_index * columns, columns + 2, axis=0
    )

    def run_clouds(clouds, halo_low, halo_high, profile, start):
        low_mean = jnp.sum(halo_low * low_mask, axis=1) / low_count
        high_mean = jnp.sum(halo_high * high_mask, axis=1) / high_count
        start_wide = jnp.concatenate((low_mean[None], start, high_mean[None]), axis=0)
        pulled = RELAXATION * (profile - start_wide)
        pulled = jnp.pad(pulled, ((0, rows - columns - 2), (0, 0)))
        clouds, sums = cloud_step(
            clouds, halo_low, halo_high, ids, bases, pulled, mix, own, up, down
        )
        return clouds, mean_of(sums, counts)

    def sent_tendency(tendency):
        coeffs = jnp.einsum("xn,xk->nk", local_table, tendency, precision=HIGH)
        coeffs = coeffs.reshape(lat_count, owned * 2, seg_count, pairs_here)
        return jnp.transpose(coeffs, (0, 2, 1, 3)).reshape(devices, flat)

    halo_low, halo_high = edges(clouds)
    clouds, after = run_clouds(clouds, halo_low, halo_high, profile, start)
    halo_low, halo_high = edges(clouds)
    sent = sent_tendency(after - start)
    mark = jnp.broadcast_to(channel_lat.astype(jnp.float32)[None, :], (devices, TILE))
    received = lax.all_to_all(
        jnp.concatenate((sent, mark), axis=1), BOTH, split_axis=0, concat_axis=0, tiled=True
    )
    source_lat = received[:, flat].astype(jnp.int32)
    to_rows, from_rows = meridian_tables(source_lat, degrees, lat_total)
    spectrum = base_spectrum + jnp.dot(to_rows, received[:, :flat], precision=HIGHEST)
    spectrum = implicit_solve(spectrum, lat_index * owned, pairs_here)

    channel_coeffs = jnp.dot(from_rows, spectrum, precision=HIGHEST)
    arrived = lax.all_to_all(channel_coeffs, BOTH, split_axis=0, concat_axis=0, tiled=True)
    arrived = arrived.reshape(lat_count, seg_count, owned * 2, pairs_here)
    arrived = jnp.transpose(arrived, (0, 2, 1, 3)).reshape(M * 2, pairs)
    profile = jnp.dot(local_inverse, arrived, precision=HIGH)
    base_spectrum = jnp.dot(there_and_back, spectrum, precision=HIGH)

    start = after
    clouds, after = run_clouds(clouds, halo_low, halo_high, profile, start)
    received = lax.all_to_all(
        sent_tendency(after - start), BOTH, split_axis=0, concat_axis=0, tiled=True
    )
    spectrum = base_spectrum + jnp.dot(to_rows, received, precision=HIGHEST)
    spectrum = implicit_solve(spectrum, lat_index * owned, pairs_here)
    back_rows = jnp.dot(from_spec, spectrum, precision=HIGH)
    restored = lax.all_to_all(back_rows, "lat", split_axis=0, concat_axis=1, tiled=True)
    atmosphere = jnp.einsum(
        "jnk,xn->jkx", restored.reshape(lat_dev, M * 2, pairs_here), inverse, precision=HIGH
    )
    return (atmosphere, clouds[None])


def solution(mesh):
    placed = (
        P("lat", "seg", None),
        P("lat", None, "seg"),
        P("lat"),
        P("lat", "seg"),
        P("lat", None),
        P(),
        P(),
    )
    return jax.shard_map(
        whole_run,
        mesh=mesh,
        in_specs=placed,
        out_specs=(P("lat", "seg", None), P("lat", None, "seg")),
        check_vma=False,
    )
```
